128 devices in a mesh: grp: 4 (over z), shard: 8 (over y_hi, x), tp: 4 (over y_lo, core).
Axes of the slice: x: 4, y: 4 (y_hi: 2, y_lo: 2; y = y_hi * 2 + y_lo), z: 4, core: 2. Of those that a mesh axis runs over, the one named last changes fastest.
Arguments:
- inner_weights: float32 [4, 2, 4096, 7168], P('grp', None, 'shard', 'tp'), may hold values from -6 to 6
- start_weights: float32 [2, 4096, 7168], P(None, 'shard', 'tp'), may hold values from -6 to 6
- momentum: float32 [2, 8, 4, 128, 4, 1792], P(None, None, None, ('grp', 'shard', 'tp')), may hold values from -6 to 6
Outputs:
- new_weights: float32 [2, 4096, 7168], P(None, 'shard', 'tp')
- new_momentum: float32 [2, 8, 4, 128, 4, 1792], P(None, None, None, ('grp', 'shard', 'tp'))
The draws below stay inside these ranges and needn't reach their ends.
All inputs are finite; a program needn't handle non-finite values.
Results may differ from the reference program's by a relative error of at most 0.00002.
Values sent between devices are 32-bit elements; how exact they have to be, the bound alone decides.
A program may use at most 128 MiB of HBM per device.

```python
import jax
import jax.numpy as jnp

D = 4096
FF = 7168
QROWS = 4
N_GRP = 4
N_SHARD = 8
N_TP = 4
DEVICES = 128


def block_levels(stream_key, dims, shards, low, high):
    def one(axis_at, shards_of):
        draws = jax.random.uniform(jax.random.fold_in(jax.random.fold_in(stream_key, 6), axis_at), (shards_of,), jnp.float32, low / len(shards), high / len(shards))
        return jnp.repeat(jnp.exp(draws), dims[axis_at] // shards_of).reshape((-1,) + (1,) * (len(dims) - axis_at - 1))

    loudness = one(*shards[0])
    for cut in shards[1:]:
        loudness = loudness * one(*cut)
    return loudness


def noise(own_key, shape, spread, most, split=(), kind=jnp.bfloat16):
    factor_of = block_levels(own_key, shape, split, -0.22, 0.18) if split else 1.0
    drawn = jax.random.normal(own_key, shape, jnp.float32) * spread * factor_of
    return jnp.minimum(jnp.maximum(drawn, -most), most).astype(kind)


def setup_inputs(seed: int = 0) -> dict:
    splits = jax.random.split(jax.random.key(seed), 4)
    inner_weights = noise(splits[0], (N_GRP, 2, D, FF), 1.0, 6.0, ((0, 4), (2, 8), (3, 4)), jnp.float32)
    start_weights = noise(splits[1], (2, D, FF), 1.0, 6.0, ((1, 8), (2, 4)), jnp.float32)
    momentum = noise(splits[2], (2, N_SHARD, N_TP, DEVICES, QROWS, FF // N_TP), 1.0, 6.0, ((3, 128),), jnp.float32)
    return {"inner_weights": inner_weights, "start_weights": start_weights, "momentum": momentum}


OUTER_RATE = 0.7
MOMENTUM_COEF = 0.5


def reference(inner_weights, start_weights, momentum):
    summed = jnp.zeros(start_weights.shape, jnp.float32)
    for member in range(N_GRP):
        summed = summed + (start_weights - inner_weights[member])
    mean_diff = summed / N_GRP
    flat_diff = mean_diff.reshape(2, N_SHARD, DEVICES, QROWS, N_TP, FF // N_TP).transpose(0, 1, 4, 2, 3, 5)
    new_momentum = MOMENTUM_COEF * momentum + flat_diff
    flat_step = OUTER_RATE * (flat_diff + MOMENTUM_COEF * new_momentum)
    update = flat_step.transpose(0, 1, 3, 4, 2, 5).reshape(2, D, FF)
    new_weights = start_weights - update
    return new_weights, new_momentum
```

```python
import functools

import jax
import jax.numpy as jnp
from jax import lax
from jax.experimental import pallas as pl
from jax.experimental.pallas import tpu as pltpu
from jax.sharding import PartitionSpec as P

OUTER_RATE = 0.7
MOMENTUM_COEF = 0.5
CHUNKS = 4
UP, DOWN = 0, 1
FAR, NEAR, RELAY, OUT_FAR, OUT_NEAR, OUT_RELAY = range(6)
MESH = pl.DeviceIdType.MESH


def kernel(
    inner, start, mom, new_w, new_mom,
    diff, base, land, mom_in, mom_out, own_w,
    load_sem, z_send, z_recv, in_send, in_recv, out_send, out_recv, local_sem,
):
    groups, shards, tps = lax.axis_size("grp"), lax.axis_size("shard"), lax.axis_size("tp")
    plane = shards * tps
    g, s, t = lax.axis_index("grp"), lax.axis_index("shard"), lax.axis_index("tp")
    me = s * tps + t
    up, down, far = (g + 1) % groups, (g + groups - 1) % groups, (g + 2) % groups
    rows = start.shape[1] // groups
    step = rows // CHUNKS
    q_rows = mom.shape[2]
    per_step = step // q_rows
    side = ((up, s, t), (down, s, t))

    def at_rows(quarter, c):
        return pl.ds(pl.multiple_of(quarter * rows + c * step, step), step)

    def in_chunk(c):
        return pl.ds(pl.multiple_of(c * step, step), step)

    def load(slot, a, quarter, begin):
        where = pl.ds(pl.multiple_of(quarter * rows, rows), rows)
        for k, (src, dst) in enumerate(((inner, diff), (start, base))):
            copy = pltpu.make_async_copy(src.at[a, where], dst.at[a, where], load_sem.at[slot, k])
            copy.start() if begin else copy.wait()

    blocks = ((0, far), (1, far), (1, up), (0, down), (0, up), (1, down), (0, g), (1, g))

    def subtract(a, quarter):
        def one(c, carry):
            where = at_rows(quarter, c)
            diff[a, where] = base[a, where] - diff[a, where]
            return carry
        lax.fori_loop(0, CHUNKS, one, 0)

    def z_copy(direction, kind, c, src, dst):
        return pltpu.make_async_remote_copy(
            src_ref=src, dst_ref=dst,
            send_sem=z_send.at[direction, kind, c], recv_sem=z_recv.at[direction, kind, c],
            device_id=side[direction], device_id_type=MESH)

    def sum_copy(direction, kind, c, quarter, a):
        slot = land.at[direction, kind, in_chunk(c)]
        return z_copy(direction, kind, c, diff.at[a, at_rows(quarter, c)], slot)

    def own_copy(direction, kind, c, a):
        return z_copy(direction, kind, c, own_w.at[a, in_chunk(c)], new_w.at[a, at_rows(g, c)])

    def relay_copy(direction, c, quarter, a):
        where = at_rows(quarter, c)
        return z_copy(direction, OUT_RELAY, c, new_w.at[a, where], new_w.at[a, where])

    def partner(k):
        other = (me + k) % plane
        return other, (g, other // tps, other % tps)

    def in_copy(k):
        other, device = partner(k)
        return pltpu.make_async_remote_copy(
            src_ref=mom.at[:, other], dst_ref=mom_in.at[:, me],
            send_sem=in_send.at[other], recv_sem=in_recv.at[me],
            device_id=device, device_id_type=MESH)

    def in_arrival(other):
        return pltpu.make_async_copy(mom_in.at[:, other], mom_in.at[:, other], in_recv.at[other])

    def out_copy(other):
        return pltpu.make_async_remote_copy(
            src_ref=mom_out.at[:, other], dst_ref=new_mom.at[:, me],
            send_sem=out_send.at[other], recv_sem=out_recv.at[me],
            device_id=(g, other // tps, other % tps), device_id_type=MESH)

    def out_arrival(other):
        return pltpu.make_async_copy(new_mom.at[:, other], new_mom.at[:, other], out_recv.at[other])

    def loop(n, body):
        def one(i, carry):
            body(i)
            return carry
        lax.fori_loop(0, n, one, 0)

    for slot in (0, 1):
        load(slot, *blocks[slot], True)

    barrier = pltpu.get_barrier_semaphore()
    for device in side:
        pl.semaphore_signal(barrier, inc=1, device_id=device, device_id_type=MESH)

    def greet(k):
        pl.semaphore_signal(barrier, inc=1, device_id=partner(k + 1)[1], device_id_type=MESH)
    loop(plane - 1, greet)
    pl.semaphore_wait(barrier, plane + 1)

    for slot in (0, 1):
        load(slot, *blocks[slot], False)

    def send_far(c):
        for a in (0, 1):
            where = at_rows(far, c)
            diff[a, where] = base[a, where] - diff[a, where]
        sum_copy(UP, FAR, c, far, 0).start()
        sum_copy(DOWN, FAR, c, far, 1).start()
    loop(CHUNKS, send_far)

    for slot in range(2, 8):
        load(slot, *blocks[slot], True)
    own_in = pltpu.make_async_copy(mom.at[:, me], mom_in.at[:, me], local_sem.at[0])
    own_in.start()
    loop(plane - 1, lambda k: in_copy(k + 1).start())

    for slot in (2, 3):
        load(slot, *blocks[slot], False)

    def send_near(c):
        for a, quarter in ((1, up), (0, down)):
            where = at_rows(quarter, c)
            diff[a, where] = base[a, where] - diff[a, where]
        sum_copy(UP, NEAR, c, up, 1).start()
        sum_copy(DOWN, NEAR, c, down, 0).start()
    loop(CHUNKS, send_near)

    for slot in range(4, 8):
        load(slot, *blocks[slot], False)
        subtract(*blocks[slot])

    def send_relay(c):
        for direction, a, quarter in ((UP, 0, up), (DOWN, 1, down)):
            sum_copy(direction, FAR, c, far, a).wait_recv()
            where = at_rows(quarter, c)
            diff[a, where] = diff[a, where] + land[direction, FAR, in_chunk(c)]
        sum_copy(UP, RELAY, c, up, 0).start()
        sum_copy(DOWN, RELAY, c, down, 1).start()
    loop(CHUNKS, send_relay)

    own_in.wait()
    loop(plane - 1, lambda k: in_arrival((me + k + 1) % plane).wait())

    def finish(c):
        for direction, near_a, relay_a in ((UP, 1, 0), (DOWN, 0, 1)):
            sum_copy(direction, NEAR, c, up, near_a).wait_recv()
            sum_copy(direction, RELAY, c, up, relay_a).wait_recv()

        def pair(i):
            for a, near, relay in ((0, DOWN, UP), (1, UP, DOWN)):
                local = pl.ds(pl.multiple_of(c * step + i * 2 * q_rows, 2 * q_rows), 2 * q_rows)
                where = pl.ds(pl.multiple_of(g * rows + c * step + i * 2 * q_rows, 2 * q_rows), 2 * q_rows)
                j = c * per_step + 2 * i
                total = diff[a, where] + land[near, NEAR, local] + land[relay, RELAY, local]
                flat = total / groups
                old = jnp.concatenate([mom_in[a, j], mom_in[a, j + 1]], axis=0)
                fresh = MOMENTUM_COEF * old + flat
                mom_out[a, j] = fresh[:q_rows]
                mom_out[a, j + 1] = fresh[q_rows:]
                own_w[a, local] = base[a, where] - OUTER_RATE * (flat + MOMENTUM_COEF * fresh)
        loop(per_step // 2, pair)
        own_copy(UP, OUT_FAR, c, 0).start()
        own_copy(DOWN, OUT_FAR, c, 1).start()
        own_copy(UP, OUT_NEAR, c, 1).start()
        own_copy(DOWN, OUT_NEAR, c, 0).start()

        def give(i):
            other = c * per_step + i

            @pl.when(other != me)
            def _():
                out_copy(other).start()
        loop(per_step, give)
    loop(CHUNKS, finish)
    mine = pl.ds(pl.multiple_of(g * rows, rows), rows)
    keep_w = pltpu.make_async_copy(own_w, new_w.at[:, mine], local_sem.at[1])
    keep_mom = pltpu.make_async_copy(mom_out.at[:, me], new_mom.at[:, me], local_sem.at[2])
    keep_w.start()
    keep_mom.start()

    def pass_on(c):
        for direction, source, a in ((UP, down, 0), (DOWN, up, 1)):
            own_copy(direction, OUT_FAR, c, a).wait_recv()
            relay_copy(direction, c, source, a).start()
    loop(CHUNKS, pass_on)

    def drain(c):
        for direction, near_a, a in ((UP, 1, 0), (DOWN, 0, 1)):
            own_copy(direction, OUT_NEAR, c, near_a).wait_recv()
            relay_copy(direction, c, far, a).wait_recv()
        for direction in (UP, DOWN):
            for kind in (FAR, NEAR, RELAY, OUT_FAR, OUT_NEAR, OUT_RELAY):
                z_copy(direction, kind, c, own_w.at[0, in_chunk(c)], own_w.at[0, in_chunk(c)]).wait_send()
    loop(CHUNKS, drain)
    keep_w.wait()
    keep_mom.wait()

    def drain_plane(k):
        other = (me + k + 1) % plane
        in_copy(k + 1).wait_send()
        out_copy(other).wait_send()
        out_arrival(other).wait()
    loop(plane - 1, drain_plane)


def body(inner_weights, start_weights, momentum):
    groups, shards, tps = lax.axis_size("grp"), lax.axis_size("shard"), lax.axis_size("tp")
    plane = shards * tps
    mats, row_count, col_count = start_weights.shape
    q_rows = momentum.shape[4]
    quarter = row_count // groups
    any_spec = pl.BlockSpec(memory_space=pl.ANY)
    flat_shape = (mats, plane, q_rows, col_count)
    dma = pltpu.SemaphoreType.DMA
    new_w, new_mom = pl.pallas_call(
        kernel,
        out_shape=(
            jax.ShapeDtypeStruct(start_weights.shape, jnp.float32),
            jax.ShapeDtypeStruct(flat_shape, jnp.float32),
        ),
        in_specs=[any_spec] * 3,
        out_specs=(any_spec, any_spec),
        scratch_shapes=[
            pltpu.VMEM(start_weights.shape, jnp.float32),
            pltpu.VMEM(start_weights.shape, jnp.float32),
            pltpu.VMEM((2, 3, quarter, col_count), jnp.float32),
            pltpu.VMEM(flat_shape, jnp.float32),
            pltpu.VMEM(flat_shape, jnp.float32),
            pltpu.VMEM((mats, quarter, col_count), jnp.float32),
            dma((8, 2)),
            dma((2, 6, CHUNKS)),
            dma((2, 6, CHUNKS)),
            dma((plane,)),
            dma((plane,)),
            dma((plane,)),
            dma((plane,)),
            dma((3,)),
        ],
        compiler_params=pltpu.CompilerParams(collective_id=0, has_side_effects=True, vmem_limit_bytes=60000000),
        name="outer_step",
    )(inner_weights[0], start_weights, momentum.reshape(flat_shape))
    return new_w, new_mom.reshape(momentum.shape)


def solution(mesh):
    in_specs = (
        P("grp", None, "shard", "tp"),
        P(None, "shard", "tp"),
        P(None, None, None, ("grp", "shard", "tp"), None, None),
    )
    out_specs = (P(None, "shard", "tp"), P(None, None, None, ("grp", "shard", "tp"), None, None))
    return jax.shard_map(body, mesh=mesh, in_specs=in_specs, out_specs=out_specs, check_vma=False)
```

```python
import functools

import jax
import jax.numpy as jnp
from jax import lax
from jax.experimental import pallas as pl
from jax.experimental.pallas import tpu as pltpu
from jax.sharding import PartitionSpec as P

OUTER_RATE = 0.7
MOMENTUM_COEF = 0.5
CHUNKS = 4
UP, DOWN = 0, 1
FAR, NEAR, RELAY, OUT_FAR, OUT_NEAR, OUT_RELAY = range(6)
MESH = pl.DeviceIdType.MESH


def kernel(
    inner, start, mom, new_w, new_mom,
    diff, base, land, mom_in, mom_out,
    load_sem, z_send, z_recv, in_send, in_recv, out_send, out_recv, local_sem, word_sem,
):
    groups, shards, tps = lax.axis_size("grp"), lax.axis_size("shard"), lax.axis_size("tp")
    plane = shards * tps
    g, s, t = lax.axis_index("grp"), lax.axis_index("shard"), lax.axis_index("tp")
    me = s * tps + t
    up, down, far = (g + 1) % groups, (g + groups - 1) % groups, (g + 2) % groups
    rows = start.shape[1] // groups
    step = rows // CHUNKS
    q_rows = mom.shape[2]
    per_step = step // q_rows
    side = ((up, s, t), (down, s, t))

    def at_rows(quarter, c):
        return pl.ds(pl.multiple_of(quarter * rows + c * step, step), step)

    def in_chunk(c):
        return pl.ds(pl.multiple_of(c * step, step), step)

    def load(slot, a, quarter, begin):
        where = pl.ds(pl.multiple_of(quarter * rows, rows), rows)
        for k, (src, dst) in enumerate(((inner, diff), (start, base))):
            copy = pltpu.make_async_copy(src.at[a, where], dst.at[a, where], load_sem.at[slot, k])
            copy.start() if begin else copy.wait()

    blocks = ((0, far), (1, far), (1, up), (0, down), (0, up), (1, down), (0, g), (1, g))

    def subtract(a, quarter):
        def one(c, carry):
            where = at_rows(quarter, c)
            diff[a, where] = base[a, where] - diff[a, where]
            return carry
        lax.fori_loop(0, CHUNKS, one, 0)

    def z_copy(direction, kind, c, src, dst):
        return pltpu.make_async_remote_copy(
            src_ref=src, dst_ref=dst,
            send_sem=z_send.at[direction, kind, c], recv_sem=z_recv.at[direction, kind, c],
            device_id=side[direction], device_id_type=MESH)

    def sum_copy(direction, kind, c, quarter, a):
        slot = land.at[direction, kind, in_chunk(c)]
        return z_copy(direction, kind, c, diff.at[a, at_rows(quarter, c)], slot)

    def own_copy(direction, kind, c, a):
        where = at_rows(g, c)
        return z_copy(direction, kind, c, new_w.at[a, where], new_w.at[a, where])

    def relay_copy(direction, c, quarter, a):
        where = at_rows(quarter, c)
        return z_copy(direction, OUT_RELAY, c, new_w.at[a, where], new_w.at[a, where])

    def partner(k):
        other = (me + k) % plane
        return other, (g, other // tps, other % tps)

    def in_copy(k):
        other, device = partner(k)
        return pltpu.make_async_remote_copy(
            src_ref=mom.at[:, other], dst_ref=mom_in.at[:, me],
            send_sem=in_send.at[other], recv_sem=in_recv.at[me],
            device_id=device, device_id_type=MESH)

    def in_arrival(other):
        return pltpu.make_async_copy(mom_in.at[:, other], mom_in.at[:, other], in_recv.at[other])

    def out_copy(other):
        return pltpu.make_async_remote_copy(
            src_ref=mom_out.at[:, other], dst_ref=new_mom.at[:, me],
            send_sem=out_send.at[other], recv_sem=out_recv.at[me],
            device_id=(g, other // tps, other % tps), device_id_type=MESH)

    def out_arrival(other):
        return pltpu.make_async_copy(new_mom.at[:, other], new_mom.at[:, other], out_recv.at[other])

    def loop(n, body):
        def one(i, carry):
            body(i)
            return carry
        lax.fori_loop(0, n, one, 0)

    for slot in (0, 1):
        load(slot, *blocks[slot], True)

    x_size, y_low = shards // 2, tps // 2
    x, y, core = s % x_size, (s // x_size) * y_low + t // 2, t % 2

    def seat(dx, dy, dcore):
        nx, ny = (x + dx + x_size) % x_size, (y + dy + 2 * y_low) % (2 * y_low)
        return (g, (ny // y_low) * x_size + nx, (ny % y_low) * 2 + (core + dcore) % 2)

    along_x, along_y, beside = (seat(1, 0, 0), seat(-1, 0, 0)), (seat(0, 1, 0), seat(0, -1, 0)), (seat(0, 0, 1),)

    barrier = pltpu.get_barrier_semaphore()
    nearest = side + along_x + along_y + beside
    for device in nearest:
        pl.semaphore_signal(barrier, inc=1, device_id=device, device_id_type=MESH)
    pl.semaphore_wait(barrier, len(nearest))

    rounds = (along_x, along_y, along_x, beside)

    def tell(i):
        for device in rounds[i]:
            pl.semaphore_signal(word_sem.at[i], inc=1, device_id=device, device_id_type=MESH)

    def hear(i):
        pl.semaphore_wait(word_sem.at[i], len(rounds[i]))

    tell(0)

    for slot in (0, 1):
        load(slot, *blocks[slot], False)

    def send_far(c):
        for a in (0, 1):
            where = at_rows(far, c)
            diff[a, where] = base[a, where] - diff[a, where]
        sum_copy(UP, FAR, c, far, 0).start()
        sum_copy(DOWN, FAR, c, far, 1).start()
    loop(CHUNKS, send_far)

    for slot in range(2, 8):
        load(slot, *blocks[slot], True)
    own_in = pltpu.make_async_copy(mom.at[:, me], mom_in.at[:, me], local_sem.at[0])
    own_in.start()
    hear(0)
    tell(1)

    for slot in (2, 3):
        load(slot, *blocks[slot], False)

    def send_near(c):
        for a, quarter in ((1, up), (0, down)):
            where = at_rows(quarter, c)
            diff[a, where] = base[a, where] - diff[a, where]
        sum_copy(UP, NEAR, c, up, 1).start()
        sum_copy(DOWN, NEAR, c, down, 0).start()
    loop(CHUNKS, send_near)

    hear(1)
    tell(2)
    for slot in (4, 5):
        load(slot, *blocks[slot], False)
        subtract(*blocks[slot])
    hear(2)
    tell(3)
    for slot in (6, 7):
        load(slot, *blocks[slot], False)
        subtract(*blocks[slot])
    hear(3)
    loop(plane - 1, lambda k: in_copy(k + 1).start())

    def send_relay(c):
        for direction, a, quarter in ((UP, 0, up), (DOWN, 1, down)):
            sum_copy(direction, FAR, c, far, a).wait_recv()
            where = at_rows(quarter, c)
            diff[a, where] = diff[a, where] + land[direction, FAR, in_chunk(c)]
        sum_copy(UP, RELAY, c, up, 0).start()
        sum_copy(DOWN, RELAY, c, down, 1).start()
    loop(CHUNKS, send_relay)

    own_in.wait()
    loop(plane - 1, lambda k: in_arrival((me + k + 1) % plane).wait())

    def finish(c):
        for direction, near_a, relay_a in ((UP, 1, 0), (DOWN, 0, 1)):
            sum_copy(direction, NEAR, c, up, near_a).wait_recv()
            sum_copy(direction, RELAY, c, up, relay_a).wait_recv()

        def pair(i):
            for a, near, relay in ((0, DOWN, UP), (1, UP, DOWN)):
                local = pl.ds(pl.multiple_of(c * step + i * 2 * q_rows, 2 * q_rows), 2 * q_rows)
                where = pl.ds(pl.multiple_of(g * rows + c * step + i * 2 * q_rows, 2 * q_rows), 2 * q_rows)
                j = c * per_step + 2 * i
                total = diff[a, where] + land[near, NEAR, local] + land[relay, RELAY, local]
                flat = total / groups
                old = jnp.concatenate([mom_in[a, j], mom_in[a, j + 1]], axis=0)
                fresh = MOMENTUM_COEF * old + flat
                mom_out[a, j] = fresh[:q_rows]
                mom_out[a, j + 1] = fresh[q_rows:]
                new_w[a, where] = base[a, where] - OUTER_RATE * (flat + MOMENTUM_COEF * fresh)
        loop(per_step // 2, pair)
        own_copy(UP, OUT_FAR, c, 0).start()
        own_copy(DOWN, OUT_FAR, c, 1).start()
        own_copy(UP, OUT_NEAR, c, 1).start()
        own_copy(DOWN, OUT_NEAR, c, 0).start()

        def give(i):
            other = c * per_step + i

            @pl.when(other != me)
            def _():
                out_copy(other).start()
        loop(per_step, give)
    loop(CHUNKS, finish)
    new_mom[:, me] = mom_out[:, me]

    def pass_on(c):
        for direction, source, a in ((UP, down, 0), (DOWN, up, 1)):
            own_copy(direction, OUT_FAR, c, a).wait_recv()
            relay_copy(direction, c, source, a).start()
    loop(CHUNKS, pass_on)

    def drain(c):
        for direction, near_a, a in ((UP, 1, 0), (DOWN, 0, 1)):
            own_copy(direction, OUT_NEAR, c, near_a).wait_recv()
            relay_copy(direction, c, far, a).wait_recv()
        for direction in (UP, DOWN):
            for kind in (FAR, NEAR, RELAY, OUT_FAR, OUT_NEAR, OUT_RELAY):
                own_copy(direction, kind, c, 0).wait_send()
    loop(CHUNKS, drain)

    def drain_plane(k):
        other = (me + k + 1) % plane
        in_copy(k + 1).wait_send()
        out_copy(other).wait_send()
        out_arrival(other).wait()
    loop(plane - 1, drain_plane)


def body(inner_weights, start_weights, momentum):
    groups, shards, tps = lax.axis_size("grp"), lax.axis_size("shard"), lax.axis_size("tp")
    plane = shards * tps
    mats, row_count, col_count = start_weights.shape
    q_rows = momentum.shape[4]
    quarter = row_count // groups
    any_spec = pl.BlockSpec(memory_space=pl.ANY)
    flat_shape = (mats, plane, q_rows, col_count)
    dma = pltpu.SemaphoreType.DMA
    new_w, new_mom = pl.pallas_call(
        kernel,
        out_shape=(
            pltpu.VMEM(start_weights.shape, jnp.float32),
            pltpu.VMEM(flat_shape, jnp.float32),
        ),
        in_specs=[any_spec] * 3,
        out_specs=(pl.BlockSpec(memory_space=pltpu.VMEM),) * 2,
        scratch_shapes=[
            pltpu.VMEM(start_weights.shape, jnp.float32),
            pltpu.VMEM(start_weights.shape, jnp.float32),
            pltpu.VMEM((2, 3, quarter, col_count), jnp.float32),
            pltpu.VMEM(flat_shape, jnp.float32),
            pltpu.VMEM(flat_shape, jnp.float32),
            dma((8, 2)),
            dma((2, 6, CHUNKS)),
            dma((2, 6, CHUNKS)),
            dma((plane,)),
            dma((plane,)),
            dma((plane,)),
            dma((plane,)),
            dma((1,)),
            pltpu.SemaphoreType.REGULAR((4,)),
        ],
        compiler_params=pltpu.CompilerParams(collective_id=0, has_side_effects=True, vmem_limit_bytes=50000000),
        name="outer_step",
    )(inner_weights[0], start_weights, momentum.reshape(flat_shape))
    return new_w, new_mom.reshape(momentum.shape)


def solution(mesh):
    in_specs = (
        P("grp", None, "shard", "tp"),
        P(None, "shard", "tp"),
        P(None, None, None, ("grp", "shard", "tp"), None, None),
    )
    out_specs = (P(None, "shard", "tp"), P(None, None, None, ("grp", "shard", "tp"), None, None))
    return jax.shard_map(body, mesh=mesh, in_specs=in_specs, out_specs=out_specs, check_vma=False)
```

```python
import functools

import jax
import jax.numpy as jnp
from jax import lax
from jax.experimental import pallas as pl
from jax.experimental.pallas import tpu as pltpu
from jax.sharding import PartitionSpec as P

OUTER_RATE = 0.7
MOMENTUM_COEF = 0.5
CHUNKS = 2
UP, DOWN = 0, 1
FAR, NEAR, RELAY, OUT_FAR, OUT_NEAR, OUT_RELAY = range(6)
MESH = pl.DeviceIdType.MESH


def kernel(
    inner, start, mom, new_w, new_mom,
    diff, base, land, mom_in, mom_out,
    load_sem, z_send, z_recv, in_send, in_recv, out_send, out_recv, local_sem, near_sem, word_sem,
):
    groups, shards, tps = lax.axis_size("grp"), lax.axis_size("shard"), lax.axis_size("tp")
    plane = shards * tps
    g, s, t = lax.axis_index("grp"), lax.axis_index("shard"), lax.axis_index("tp")
    me = s * tps + t
    up, down, far = (g + 1) % groups, (g + groups - 1) % groups, (g + 2) % groups
    rows = start.shape[1] // groups
    step = rows // CHUNKS
    q_rows = mom.shape[2]
    per_step = step // q_rows
    side = ((up, s, t), (down, s, t))

    def at_rows(quarter, c):
        return pl.ds(pl.multiple_of(quarter * rows + c * step, step), step)

    def in_chunk(c):
        return pl.ds(pl.multiple_of(c * step, step), step)

    def load(slot, a, quarter, begin):
        where = pl.ds(pl.multiple_of(quarter * rows, rows), rows)
        for k, (src, dst) in enumerate(((inner, diff), (start, base))):
            copy = pltpu.make_async_copy(src.at[a, where], dst.at[a, where], load_sem.at[slot, k])
            copy.start() if begin else copy.wait()

    blocks = ((0, up), (1, down), (0, g), (1, g))

    def subtract(a, quarter):
        def one(c, carry):
            where = at_rows(quarter, c)
            diff[a, where] = base[a, where] - diff[a, where]
            return carry
        lax.fori_loop(0, CHUNKS, one, 0)

    def z_copy(direction, kind, c, src, dst):
        return pltpu.make_async_remote_copy(
            src_ref=src, dst_ref=dst,
            send_sem=z_send.at[direction, kind, c], recv_sem=z_recv.at[direction, kind, c],
            device_id=side[direction], device_id_type=MESH)

    def sum_copy(direction, kind, c, quarter, a):
        source = diff if kind == RELAY else inner
        slot = land.at[direction, kind, in_chunk(c)]
        return z_copy(direction, kind, c, source.at[a, at_rows(quarter, c)], slot)

    def own_copy(direction, kind, c, a):
        where = at_rows(g, c)
        return z_copy(direction, kind, c, new_w.at[a, where], new_w.at[a, where])

    def relay_copy(direction, c, quarter, a):
        where = at_rows(quarter, c)
        return z_copy(direction, OUT_RELAY, c, new_w.at[a, where], new_w.at[a, where])

    def partner(k):
        other = (me + k) % plane
        return other, (g, other // tps, other % tps)

    def in_copy(k):
        other, device = partner(k)
        return pltpu.make_async_remote_copy(
            src_ref=mom.at[:, other], dst_ref=mom_in.at[:, me],
            send_sem=in_send.at[other], recv_sem=in_recv.at[me],
            device_id=device, device_id_type=MESH)

    def in_arrival(other):
        return pltpu.make_async_copy(mom_in.at[:, other], mom_in.at[:, other], in_recv.at[other])

    def out_copy(other):
        return pltpu.make_async_remote_copy(
            src_ref=mom_out.at[:, other], dst_ref=new_mom.at[:, me],
            send_sem=out_send.at[other], recv_sem=out_recv.at[me],
            device_id=(g, other // tps, other % tps), device_id_type=MESH)

    def out_arrival(other):
        return pltpu.make_async_copy(new_mom.at[:, other], new_mom.at[:, other], out_recv.at[other])

    def loop(n, body):
        def one(i, carry):
            body(i)
            return carry
        lax.fori_loop(0, n, one, 0)

    x_size, y_low = shards // 2, tps // 2
    x, y, core = s % x_size, (s // x_size) * y_low + t // 2, t % 2

    def seat(dx, dy, dcore):
        nx, ny = (x + dx + x_size) % x_size, (y + dy + 2 * y_low) % (2 * y_low)
        return (g, (ny // y_low) * x_size + nx, (ny % y_low) * 2 + (core + dcore) % 2)

    along_x, along_y, beside = (seat(1, 0, 0), seat(-1, 0, 0)), (seat(0, 1, 0), seat(0, -1, 0)), (seat(0, 0, 1),)

    def signal(sem, *devices):
        for device in devices:
            pl.semaphore_signal(sem, inc=1, device_id=device, device_id_type=MESH)

    barrier = pltpu.get_barrier_semaphore()

    @pl.when(g == 0)
    def _():
        signal(barrier, *side, *along_x, *along_y, *beside)

    @pl.when(g == 1)
    def _():
        signal(barrier, side[UP])

    @pl.when(g == 3)
    def _():
        signal(barrier, side[DOWN])
    pl.semaphore_wait(barrier, jnp.where(g == 0, 5, jnp.where(g == 2, 2, 1)))

    @pl.when((g == 1) | (g == 2))
    def _():
        signal(near_sem.at[UP], side[DOWN])

    @pl.when((g == 3) | (g == 2))
    def _():
        signal(near_sem.at[DOWN], side[UP])

    def send_raw(direction, a, owner):
        loop(CHUNKS, lambda c: sum_copy(direction, FAR, c, far, a).start())
        loop(CHUNKS, lambda c: sum_copy(direction, NEAR, c, owner, 1 - a).start())

    @pl.when(g == 1)
    def _():
        send_raw(DOWN, 1, down)

    @pl.when(g < 2)
    def _():
        pl.semaphore_wait(near_sem.at[UP], 1)
    send_raw(UP, 0, up)

    @pl.when((g == 0) | (g == 3))
    def _():
        pl.semaphore_wait(near_sem.at[DOWN], 1)

    @pl.when(g != 1)
    def _():
        send_raw(DOWN, 1, down)

    @pl.when(g == 1)
    def _():
        signal(word_sem.at[0], side[DOWN])

    rounds = (along_x, along_y, along_x, along_y, beside)

    def hear(i):
        @pl.when(g == 0)
        def _():
            pl.semaphore_wait(word_sem.at[i], 1 if i == 0 else len(rounds[i - 1]))
            if i < len(rounds):
                signal(word_sem.at[i + 1], *rounds[i])
            else:
                signal(word_sem.at[i + 1], (up, s, t), (far, s, t), (down, s, t))

    for slot in range(4):
        load(slot, *blocks[slot], True)
    own_in = pltpu.make_async_copy(mom.at[:, me], mom_in.at[:, me], local_sem.at[0])
    own_in.start()

    hear(0)
    for slot in range(4):
        load(slot, *blocks[slot], False)
        subtract(*blocks[slot])
        hear(slot + 1)
    hear(5)

    @pl.when(g != 0)
    def _():
        pl.semaphore_wait(word_sem.at[6], 1)
    loop(plane - 1, lambda k: in_copy(k + 1).start())

    def send_relay(c):
        for direction, a, quarter in ((UP, 0, up), (DOWN, 1, down)):
            sum_copy(direction, FAR, c, far, a).wait_recv()
            where = at_rows(quarter, c)
            diff[a, where] = diff[a, where] + (base[a, where] - land[direction, FAR, in_chunk(c)])
        sum_copy(UP, RELAY, c, up, 0).start()
        sum_copy(DOWN, RELAY, c, down, 1).start()
    loop(CHUNKS, send_relay)

    own_in.wait()
    loop(plane - 1, lambda k: in_arrival((me + k + 1) % plane).wait())

    def finish(c):
        for direction, near_a, relay_a in ((UP, 1, 0), (DOWN, 0, 1)):
            sum_copy(direction, NEAR, c, up, near_a).wait_recv()
            sum_copy(direction, RELAY, c, up, relay_a).wait_recv()

        def pair(i):
            for a, near, relay in ((0, DOWN, UP), (1, UP, DOWN)):
                local = pl.ds(pl.multiple_of(c * step + i * 2 * q_rows, 2 * q_rows), 2 * q_rows)
                where = pl.ds(pl.multiple_of(g * rows + c * step + i * 2 * q_rows, 2 * q_rows), 2 * q_rows)
                j = c * per_step + 2 * i
                total = diff[a, where] + (base[a, where] - land[near, NEAR, local]) + land[relay, RELAY, local]
                flat = total / groups
                old = jnp.concatenate([mom_in[a, j], mom_in[a, j + 1]], axis=0)
                fresh = MOMENTUM_COEF * old + flat
                mom_out[a, j] = fresh[:q_rows]
                mom_out[a, j + 1] = fresh[q_rows:]
                new_w[a, where] = base[a, where] - OUTER_RATE * (flat + MOMENTUM_COEF * fresh)
        loop(per_step // 2, pair)
        own_copy(UP, OUT_FAR, c, 0).start()
        own_copy(DOWN, OUT_FAR, c, 1).start()
        own_copy(UP, OUT_NEAR, c, 1).start()
        own_copy(DOWN, OUT_NEAR, c, 0).start()

        def give(i):
            other = c * per_step + i

            @pl.when(other != me)
            def _():
                out_copy(other).start()
        loop(per_step, give)
    loop(CHUNKS, finish)
    new_mom[:, me] = mom_out[:, me]

    def pass_on(c):
        for direction, source, a in ((UP, down, 0), (DOWN, up, 1)):
            own_copy(direction, OUT_FAR, c, a).wait_recv()
            relay_copy(direction, c, source, a).start()
    loop(CHUNKS, pass_on)

    def drain(c):
        for direction, near_a, a in ((UP, 1, 0), (DOWN, 0, 1)):
            own_copy(direction, OUT_NEAR, c, near_a).wait_recv()
            relay_copy(direction, c, far, a).wait_recv()
        for direction in (UP, DOWN):
            for kind in (FAR, NEAR, RELAY, OUT_FAR, OUT_NEAR, OUT_RELAY):
                own_copy(direction, kind, c, 0).wait_send()
    loop(CHUNKS, drain)

    def drain_plane(k):
        other = (me + k + 1) % plane
        in_copy(k + 1).wait_send()
        out_copy(other).wait_send()
        out_arrival(other).wait()
    loop(plane - 1, drain_plane)


def write_out(new_w, new_mom, out_w, out_mom, sem):
    copies = []
    for a in range(new_w.shape[0]):
        half = new_w.shape[1] // 2
        for part in range(2):
            where = (a, pl.ds(part * half, half))
            copies.append(pltpu.make_async_copy(new_w.at[where], out_w.at[where], sem.at[len(copies)]))
        copies.append(pltpu.make_async_copy(new_mom.at[a], out_mom.at[a], sem.at[len(copies)]))
    for copy in copies:
        copy.start()
    for copy in copies:
        copy.wait()


def body(inner_weights, start_weights, momentum):
    groups, shards, tps = lax.axis_size("grp"), lax.axis_size("shard"), lax.axis_size("tp")
    plane = shards * tps
    mats, row_count, col_count = start_weights.shape
    q_rows = momentum.shape[4]
    quarter = row_count // groups
    any_spec = pl.BlockSpec(memory_space=pl.ANY)
    flat_shape = (mats, plane, q_rows, col_count)
    dma = pltpu.SemaphoreType.DMA
    new_w, new_mom = pl.pallas_call(
        kernel,
        out_shape=(
            pltpu.VMEM(start_weights.shape, jnp.float32),
            pltpu.VMEM(flat_shape, jnp.float32),
        ),
        in_specs=[any_spec] * 3,
        out_specs=(pl.BlockSpec(memory_space=pltpu.VMEM),) * 2,
        scratch_shapes=[
            pltpu.VMEM(start_weights.shape, jnp.float32),
            pltpu.VMEM(start_weights.shape, jnp.float32),
            pltpu.VMEM((2, 3, quarter, col_count), jnp.float32),
            pltpu.VMEM(flat_shape, jnp.float32),
            pltpu.VMEM(flat_shape, jnp.float32),
            dma((4, 2)),
            dma((2, 6, CHUNKS)),
            dma((2, 6, CHUNKS)),
            dma((plane,)),
            dma((plane,)),
            dma((plane,)),
            dma((plane,)),
            dma((1,)),
            pltpu.SemaphoreType.REGULAR((2,)),
            pltpu.SemaphoreType.REGULAR((7,)),
        ],
        compiler_params=pltpu.CompilerParams(collective_id=0, has_side_effects=True, vmem_limit_bytes=50000000),
        name="outer_step",
    )(inner_weights[0], start_weights, momentum.reshape(flat_shape))
    vmem_spec = pl.BlockSpec(memory_space=pltpu.VMEM)
    out_w, out_mom = pl.pallas_call(
        write_out,
        out_shape=(
            jax.ShapeDtypeStruct(start_weights.shape, jnp.float32),
            jax.ShapeDtypeStruct(flat_shape, jnp.float32),
        ),
        in_specs=[vmem_spec] * 2,
        out_specs=(any_spec, any_spec),
        scratch_shapes=[dma((6,))],
        compiler_params=pltpu.CompilerParams(vmem_limit_bytes=4000000),
        name="write_out",
    )(new_w, new_mom)
    return out_w, out_mom.reshape(momentum.shape)


def solution(mesh):
    in_specs = (
        P("grp", None, "shard", "tp"),
        P(None, "shard", "tp"),
        P(None, None, None, ("grp", "shard", "tp"), None, None),
    )
    out_specs = (P(None, "shard", "tp"), P(None, None, None, ("grp", "shard", "tp"), None, None))
    return jax.shard_map(body, mesh=mesh, in_specs=in_specs, out_specs=out_specs, check_vma=False)
```

```python
import functools

import jax
import jax.numpy as jnp
from jax import lax
from jax.experimental import pallas as pl
from jax.experimental.pallas import tpu as pltpu
from jax.sharding import PartitionSpec as P

OUTER_RATE = 0.7
MOMENTUM_COEF = 0.5
CHUNKS = 2
UP, DOWN = 0, 1
FAR, NEAR, RELAY, OUT_FAR, OUT_NEAR, OUT_RELAY = range(6)
MESH = pl.DeviceIdType.MESH


def kernel(
    inner, start, mom, new_w, new_mom,
    diff, base, land, mom_in, mom_out,
    load_sem, z_send, z_recv, in_send, in_recv, out_send, out_recv, local_sem, near_sem, word_sem,
):
    groups, shards, tps = lax.axis_size("grp"), lax.axis_size("shard"), lax.axis_size("tp")
    plane = shards * tps
    g, s, t = lax.axis_index("grp"), lax.axis_index("shard"), lax.axis_index("tp")
    me = s * tps + t
    up, down, far = (g + 1) % groups, (g + groups - 1) % groups, (g + 2) % groups
    rows = start.shape[1] // groups
    step = rows // CHUNKS
    q_rows = mom.shape[2]
    per_step = step // q_rows
    side = ((up, s, t), (down, s, t))

    def at_rows(quarter, c):
        return pl.ds(pl.multiple_of(quarter * rows + c * step, step), step)

    def in_chunk(c):
        return pl.ds(pl.multiple_of(c * step, step), step)

    def load(slot, a, quarter, begin):
        where = pl.ds(pl.multiple_of(quarter * rows, rows), rows)
        for k, (src, dst) in enumerate(((inner, diff), (start, base))):
            copy = pltpu.make_async_copy(src.at[a, where], dst.at[a, where], load_sem.at[slot, k])
            copy.start() if begin else copy.wait()

    blocks = ((0, up), (1, down), (0, g), (1, g))

    def subtract(a, quarter):
        def one(c, carry):
            where = at_rows(quarter, c)
            diff[a, where] = base[a, where] - diff[a, where]
            return carry
        lax.fori_loop(0, CHUNKS, one, 0)

    def z_copy(direction, kind, c, src, dst):
        return pltpu.make_async_remote_copy(
            src_ref=src, dst_ref=dst,
            send_sem=z_send.at[direction, kind, c], recv_sem=z_recv.at[direction, kind, c],
            device_id=side[direction], device_id_type=MESH)

    def sum_copy(direction, kind, c, quarter, a):
        source = diff if kind == RELAY else inner
        slot = land.at[direction, kind, in_chunk(c)]
        return z_copy(direction, kind, c, source.at[a, at_rows(quarter, c)], slot)

    def own_copy(direction, kind, c, a):
        where = at_rows(g, c)
        return z_copy(direction, kind, c, new_w.at[a, where], new_w.at[a, where])

    def relay_copy(direction, c, quarter, a):
        where = at_rows(quarter, c)
        return z_copy(direction, OUT_RELAY, c, new_w.at[a, where], new_w.at[a, where])

    def partner(k):
        other = (me + k) % plane
        return other, (g, other // tps, other % tps)

    def in_copy(k):
        other, device = partner(k)
        return pltpu.make_async_remote_copy(
            src_ref=mom.at[:, other], dst_ref=mom_in.at[:, me],
            send_sem=in_send.at[other], recv_sem=in_recv.at[me],
            device_id=device, device_id_type=MESH)

    def in_arrival(other):
        return pltpu.make_async_copy(mom_in.at[:, other], mom_in.at[:, other], in_recv.at[other])

    def out_copy(other):
        return pltpu.make_async_remote_copy(
            src_ref=mom_out.at[:, other], dst_ref=new_mom.at[:, me],
            send_sem=out_send.at[other], recv_sem=out_recv.at[me],
            device_id=(g, other // tps, other % tps), device_id_type=MESH)

    def out_arrival(other):
        return pltpu.make_async_copy(new_mom.at[:, other], new_mom.at[:, other], out_recv.at[other])

    def loop(n, body):
        def one(i, carry):
            body(i)
            return carry
        lax.fori_loop(0, n, one, 0)

    x_size, y_low = shards // 2, tps // 2
    x, y, core = s % x_size, (s // x_size) * y_low + t // 2, t % 2

    def seat(dx, dy, dcore):
        nx, ny = (x + dx + x_size) % x_size, (y + dy + 2 * y_low) % (2 * y_low)
        return (g, (ny // y_low) * x_size + nx, (ny % y_low) * 2 + (core + dcore) % 2)

    along_x, along_y, beside = (seat(1, 0, 0), seat(-1, 0, 0)), (seat(0, 1, 0), seat(0, -1, 0)), (seat(0, 0, 1),)

    def signal(sem, *devices):
        for device in devices:
            pl.semaphore_signal(sem, inc=1, device_id=device, device_id_type=MESH)

    barrier = pltpu.get_barrier_semaphore()

    @pl.when(g == 0)
    def _():
        signal(barrier, *side, *along_x, *along_y, *beside)

    @pl.when(g == 1)
    def _():
        signal(barrier, side[UP])

    @pl.when(g == 3)
    def _():
        signal(barrier, side[DOWN])
    pl.semaphore_wait(barrier, jnp.where(g == 0, 5, jnp.where(g == 2, 2, 1)))

    @pl.when((g == 1) | (g == 2))
    def _():
        signal(near_sem.at[UP], side[DOWN])

    @pl.when((g == 3) | (g == 2))
    def _():
        signal(near_sem.at[DOWN], side[UP])

    def send_raw(direction, a, owner):
        loop(CHUNKS, lambda c: sum_copy(direction, FAR, c, far, a).start())
        loop(CHUNKS, lambda c: sum_copy(direction, NEAR, c, owner, 1 - a).start())

    @pl.when(g == 1)
    def _():
        send_raw(DOWN, 1, down)

    @pl.when(g < 2)
    def _():
        pl.semaphore_wait(near_sem.at[UP], 1)
    send_raw(UP, 0, up)

    @pl.when((g == 0) | (g == 3))
    def _():
        pl.semaphore_wait(near_sem.at[DOWN], 1)

    @pl.when(g != 1)
    def _():
        send_raw(DOWN, 1, down)

    @pl.when(g == 1)
    def _():
        signal(word_sem.at[0], side[DOWN])

    rounds = (along_x, along_y, along_x, along_y, beside)

    def hear(i):
        @pl.when(g == 0)
        def _():
            pl.semaphore_wait(word_sem.at[i], 1 if i == 0 else len(rounds[i - 1]))
            if i < len(rounds):
                signal(word_sem.at[i + 1], *rounds[i])
            else:
                signal(word_sem.at[i + 1], (up, s, t), (far, s, t), (down, s, t))

    for slot in range(4):
        load(slot, *blocks[slot], True)
    own_in = pltpu.make_async_copy(mom.at[:, me], mom_in.at[:, me], local_sem.at[0])
    own_in.start()

    hear(0)
    for slot in range(4):
        load(slot, *blocks[slot], False)
        subtract(*blocks[slot])
        hear(slot + 1)
    hear(5)

    @pl.when(g != 0)
    def _():
        pl.semaphore_wait(word_sem.at[6], 1)
    loop(plane - 1, lambda k: in_copy(k + 1).start())

    def send_relay(c):
        for direction, a, quarter in ((UP, 0, up), (DOWN, 1, down)):
            sum_copy(direction, FAR, c, far, a).wait_recv()
            where = at_rows(quarter, c)
            diff[a, where] = diff[a, where] + (base[a, where] - land[direction, FAR, in_chunk(c)])
        sum_copy(UP, RELAY, c, up, 0).start()
        sum_copy(DOWN, RELAY, c, down, 1).start()
    loop(CHUNKS, send_relay)

    own_in.wait()
    loop(plane - 1, lambda k: in_arrival((me + k + 1) % plane).wait())

    def finish(c):
        for direction, near_a, relay_a in ((UP, 1, 0), (DOWN, 0, 1)):
            sum_copy(direction, NEAR, c, up, near_a).wait_recv()
            sum_copy(direction, RELAY, c, up, relay_a).wait_recv()

        def pair(i):
            for a, near, relay in ((0, DOWN, UP), (1, UP, DOWN)):
                local = pl.ds(pl.multiple_of(c * step + i * 2 * q_rows, 2 * q_rows), 2 * q_rows)
                where = pl.ds(pl.multiple_of(g * rows + c * step + i * 2 * q_rows, 2 * q_rows), 2 * q_rows)
                j = c * per_step + 2 * i
                total = diff[a, where] + (base[a, where] - land[near, NEAR, local]) + land[relay, RELAY, local]
                flat = total / groups
                old = jnp.concatenate([mom_in[a, j], mom_in[a, j + 1]], axis=0)
                fresh = MOMENTUM_COEF * old + flat
                mom_out[a, j] = fresh[:q_rows]
                mom_out[a, j + 1] = fresh[q_rows:]
                new_w[a, where] = base[a, where] - OUTER_RATE * (flat + MOMENTUM_COEF * fresh)
        loop(per_step // 2, pair)
        own_copy(UP, OUT_FAR, c, 0).start()
        own_copy(DOWN, OUT_FAR, c, 1).start()
        own_copy(UP, OUT_NEAR, c, 1).start()
        own_copy(DOWN, OUT_NEAR, c, 0).start()

        def give(i):
            other = c * per_step + i

            @pl.when(other != me)
            def _():
                out_copy(other).start()
        loop(per_step, give)
    loop(CHUNKS, finish)
    new_mom[:, me] = mom_out[:, me]

    def pass_on(c):
        for direction, source, a in ((UP, down, 0), (DOWN, up, 1)):
            own_copy(direction, OUT_FAR, c, a).wait_recv()
            relay_copy(direction, c, source, a).start()
    loop(CHUNKS, pass_on)

    def drain_plane(k):
        other = (me + k + 1) % plane
        in_copy(k + 1).wait_send()
        out_copy(other).wait_send()
        out_arrival(other).wait()
    loop(plane - 1, drain_plane)

    def sent(c, *kinds):
        for kind in kinds:
            for direction in (UP, DOWN):
                own_copy(direction, kind, c, 0).wait_send()

    def arrived(c):
        for direction, a in ((UP, 1), (DOWN, 0)):
            own_copy(direction, OUT_NEAR, c, a).wait_recv()

    loop(CHUNKS, lambda c: sent(c, FAR, NEAR, RELAY, OUT_FAR, OUT_NEAR))
    loop(CHUNKS, arrived)

    def drain(c):
        sent(c, OUT_RELAY)
        for direction, a in ((UP, 0), (DOWN, 1)):
            relay_copy(direction, c, far, a).wait_recv()
    loop(CHUNKS, drain)


def write_out(new_w, new_mom, out_w, out_mom, sem):
    copies = []
    for a in range(new_w.shape[0]):
        half = new_w.shape[1] // 2
        for part in range(2):
            where = (a, pl.ds(part * half, half))
            copies.append(pltpu.make_async_copy(new_w.at[where], out_w.at[where], sem.at[len(copies)]))
        copies.append(pltpu.make_async_copy(new_mom.at[a], out_mom.at[a], sem.at[len(copies)]))
    for copy in copies:
        copy.start()
    for copy in copies:
        copy.wait()


def body(inner_weights, start_weights, momentum):
    groups, shards, tps = lax.axis_size("grp"), lax.axis_size("shard"), lax.axis_size("tp")
    plane = shards * tps
    mats, row_count, col_count = start_weights.shape
    q_rows = momentum.shape[4]
    quarter = row_count // groups
    any_spec = pl.BlockSpec(memory_space=pl.ANY)
    flat_shape = (mats, plane, q_rows, col_count)
    dma = pltpu.SemaphoreType.DMA
    new_w, new_mom = pl.pallas_call(
        kernel,
        out_shape=(
            pltpu.VMEM(start_weights.shape, jnp.float32),
            pltpu.VMEM(flat_shape, jnp.float32),
        ),
        in_specs=[any_spec] * 3,
        out_specs=(pl.BlockSpec(memory_space=pltpu.VMEM),) * 2,
        scratch_shapes=[
            pltpu.VMEM(start_weights.shape, jnp.float32),
            pltpu.VMEM(start_weights.shape, jnp.float32),
            pltpu.VMEM((2, 3, quarter, col_count), jnp.float32),
            pltpu.VMEM(flat_shape, jnp.float32),
            pltpu.VMEM(flat_shape, jnp.float32),
            dma((4, 2)),
            dma((2, 6, CHUNKS)),
            dma((2, 6, CHUNKS)),
            dma((plane,)),
            dma((plane,)),
            dma((plane,)),
            dma((plane,)),
            dma((1,)),
            pltpu.SemaphoreType.REGULAR((2,)),
            pltpu.SemaphoreType.REGULAR((7,)),
        ],
        compiler_params=pltpu.CompilerParams(collective_id=0, has_side_effects=True, vmem_limit_bytes=50000000),
        name="outer_step",
    )(inner_weights[0], start_weights, momentum.reshape(flat_shape))
    vmem_spec = pl.BlockSpec(memory_space=pltpu.VMEM)
    out_w, out_mom = pl.pallas_call(
        write_out,
        out_shape=(
            jax.ShapeDtypeStruct(start_weights.shape, jnp.float32),
            jax.ShapeDtypeStruct(flat_shape, jnp.float32),
        ),
        in_specs=[vmem_spec] * 2,
        out_specs=(any_spec, any_spec),
        scratch_shapes=[dma((6,))],
        compiler_params=pltpu.CompilerParams(vmem_limit_bytes=4000000),
        name="write_out",
    )(new_w, new_mom)
    return out_w, out_mom.reshape(momentum.shape)


def solution(mesh):
    in_specs = (
        P("grp", None, "shard", "tp"),
        P(None, "shard", "tp"),
        P(None, None, None, ("grp", "shard", "tp"), None, None),
    )
    out_specs = (P(None, "shard", "tp"), P(None, None, None, ("grp", "shard", "tp"), None, None))
    return jax.shard_map(body, mesh=mesh, in_specs=in_specs, out_specs=out_specs, check_vma=False)
```

```python
import functools

import jax
import jax.numpy as jnp
from jax import lax
from jax.experimental import pallas as pl
from jax.experimental.pallas import tpu as pltpu
from jax.sharding import PartitionSpec as P

OUTER_RATE = 0.7
MOMENTUM_COEF = 0.5
CHUNKS = 2
UP, DOWN = 0, 1
FAR, NEAR, RELAY, OUT_FAR, OUT_NEAR, OUT_RELAY = range(6)
MESH = pl.DeviceIdType.MESH


def kernel(
    inner, start, mom, new_w, new_mom,
    diff, base, land, mom_in, mom_out,
    load_sem, z_send, z_recv, plane_sem, local_sem, near_sem, word_sem,
):
    groups, shards, tps = lax.axis_size("grp"), lax.axis_size("shard"), lax.axis_size("tp")
    plane = shards * tps
    g, s, t = lax.axis_index("grp"), lax.axis_index("shard"), lax.axis_index("tp")
    me = s * tps + t
    up, down, far = (g + 1) % groups, (g + groups - 1) % groups, (g + 2) % groups
    rows = start.shape[1] // groups
    step = rows // CHUNKS
    q_rows = mom.shape[2]
    per_step = step // q_rows
    side = ((up, s, t), (down, s, t))

    def at_rows(quarter, c):
        return pl.ds(pl.multiple_of(quarter * rows + c * step, step), step)

    def in_chunk(c):
        return pl.ds(pl.multiple_of(c * step, step), step)

    def load(slot, a, quarter, begin):
        where = pl.ds(pl.multiple_of(quarter * rows, rows), rows)
        for k, (src, dst) in enumerate(((inner, diff), (start, base))):
            copy = pltpu.make_async_copy(src.at[a, where], dst.at[a, where], load_sem.at[slot, k])
            copy.start() if begin else copy.wait()

    blocks = ((0, up), (1, down), (0, g), (1, g))

    def subtract(a, quarter):
        def one(c, carry):
            where = at_rows(quarter, c)
            diff[a, where] = base[a, where] - diff[a, where]
            return carry
        lax.fori_loop(0, CHUNKS, one, 0)

    def z_copy(direction, kind, c, src, dst):
        return pltpu.make_async_remote_copy(
            src_ref=src, dst_ref=dst,
            send_sem=z_send.at[direction], recv_sem=z_recv.at[direction, kind, c],
            device_id=side[direction], device_id_type=MESH)

    def sum_copy(direction, kind, c, quarter, a):
        source = diff if kind == RELAY else inner
        slot = land.at[direction, kind, in_chunk(c)]
        return z_copy(direction, kind, c, source.at[a, at_rows(quarter, c)], slot)

    def own_copy(direction, kind, c, a):
        where = at_rows(g, c)
        return z_copy(direction, kind, c, new_w.at[a, where], new_w.at[a, where])

    def relay_copy(direction, c, quarter, a):
        where = at_rows(quarter, c)
        return z_copy(direction, OUT_RELAY, c, new_w.at[a, where], new_w.at[a, where])

    def partner(k):
        other = (me + k) % plane
        return other, (g, other // tps, other % tps)

    def in_copy(k):
        other, device = partner(k)
        return pltpu.make_async_remote_copy(
            src_ref=mom.at[:, other], dst_ref=mom_in.at[:, me],
            send_sem=plane_sem.at[0], recv_sem=plane_sem.at[1],
            device_id=device, device_id_type=MESH)

    def wait_all(ref, sem):
        pltpu.make_async_copy(ref, ref, sem).wait()

    def wait_plane(i):
        wait_all(mom_out.at[:, pl.ds(0, plane - 1)], plane_sem.at[i])

    def out_copy(other):
        return pltpu.make_async_remote_copy(
            src_ref=mom_out.at[:, other], dst_ref=new_mom.at[:, me],
            send_sem=plane_sem.at[2], recv_sem=plane_sem.at[3],
            device_id=(g, other // tps, other % tps), device_id_type=MESH)

    def loop(n, body):
        def one(i, carry):
            body(i)
            return carry
        lax.fori_loop(0, n, one, 0)

    x_size, y_low = shards // 2, tps // 2
    x, y, core = s % x_size, (s // x_size) * y_low + t // 2, t % 2

    def seat(dx, dy, dcore):
        nx, ny = (x + dx + x_size) % x_size, (y + dy + 2 * y_low) % (2 * y_low)
        return (g, (ny // y_low) * x_size + nx, (ny % y_low) * 2 + (core + dcore) % 2)

    along_x, along_y, beside = (seat(1, 0, 0), seat(-1, 0, 0)), (seat(0, 1, 0), seat(0, -1, 0)), (seat(0, 0, 1),)

    def signal(sem, *devices):
        for device in devices:
            pl.semaphore_signal(sem, inc=1, device_id=device, device_id_type=MESH)

    barrier = pltpu.get_barrier_semaphore()

    @pl.when(g == 0)
    def _():
        signal(barrier, *side, *along_x, *along_y, *beside)

    @pl.when(g == 1)
    def _():
        signal(barrier, side[UP])

    @pl.when(g == 3)
    def _():
        signal(barrier, side[DOWN])
    pl.semaphore_wait(barrier, jnp.where(g == 0, 5, jnp.where(g == 2, 2, 1)))

    @pl.when((g == 1) | (g == 2))
    def _():
        signal(near_sem.at[UP], side[DOWN])

    @pl.when((g == 3) | (g == 2))
    def _():
        signal(near_sem.at[DOWN], side[UP])

    def send_raw(direction, a, owner):
        loop(CHUNKS, lambda c: sum_copy(direction, FAR, c, far, a).start())
        loop(CHUNKS, lambda c: sum_copy(direction, NEAR, c, owner, 1 - a).start())

    @pl.when(g == 1)
    def _():
        send_raw(DOWN, 1, down)

    @pl.when(g < 2)
    def _():
        pl.semaphore_wait(near_sem.at[UP], 1)
    send_raw(UP, 0, up)

    @pl.when((g == 0) | (g == 3))
    def _():
        pl.semaphore_wait(near_sem.at[DOWN], 1)

    @pl.when(g != 1)
    def _():
        send_raw(DOWN, 1, down)

    @pl.when(g == 1)
    def _():
        signal(word_sem.at[0], side[DOWN])

    rounds = (along_x, along_y, along_x, along_y, beside)

    def hear(i):
        @pl.when(g == 0)
        def _():
            pl.semaphore_wait(word_sem.at[i], 1 if i == 0 else len(rounds[i - 1]))
            if i < len(rounds):
                signal(word_sem.at[i + 1], *rounds[i])
            else:
                signal(word_sem.at[i + 1], (up, s, t), (far, s, t), (down, s, t))

    for slot in range(4):
        load(slot, *blocks[slot], True)
    own_in = pltpu.make_async_copy(mom.at[:, me], mom_in.at[:, me], local_sem.at[0])
    own_in.start()

    hear(0)
    for slot in range(4):
        load(slot, *blocks[slot], False)
        subtract(*blocks[slot])
        hear(slot + 1)
    hear(5)

    @pl.when(g != 0)
    def _():
        pl.semaphore_wait(word_sem.at[6], 1)
    loop(plane - 1, lambda k: in_copy(k + 1).start())

    def send_relay(c):
        for direction, a, quarter in ((UP, 0, up), (DOWN, 1, down)):
            sum_copy(direction, FAR, c, far, a).wait_recv()
            where = at_rows(quarter, c)
            diff[a, where] = diff[a, where] + (base[a, where] - land[direction, FAR, in_chunk(c)])
        sum_copy(UP, RELAY, c, up, 0).start()
        sum_copy(DOWN, RELAY, c, down, 1).start()
    loop(CHUNKS, send_relay)

    own_in.wait()
    wait_plane(1)

    def finish(c):
        for direction, near_a, relay_a in ((UP, 1, 0), (DOWN, 0, 1)):
            sum_copy(direction, NEAR, c, up, near_a).wait_recv()
            sum_copy(direction, RELAY, c, up, relay_a).wait_recv()

        def pair(i):
            for a, near, relay in ((0, DOWN, UP), (1, UP, DOWN)):
                local = pl.ds(pl.multiple_of(c * step + i * 2 * q_rows, 2 * q_rows), 2 * q_rows)
                where = pl.ds(pl.multiple_of(g * rows + c * step + i * 2 * q_rows, 2 * q_rows), 2 * q_rows)
                j = c * per_step + 2 * i
                total = diff[a, where] + (base[a, where] - land[near, NEAR, local]) + land[relay, RELAY, local]
                flat = total / groups
                old = jnp.concatenate([mom_in[a, j], mom_in[a, j + 1]], axis=0)
                fresh = MOMENTUM_COEF * old + flat
                mom_out[a, j] = fresh[:q_rows]
                mom_out[a, j + 1] = fresh[q_rows:]
                new_w[a, where] = base[a, where] - OUTER_RATE * (flat + MOMENTUM_COEF * fresh)
        loop(per_step // 2, pair)
        own_copy(UP, OUT_FAR, c, 0).start()
        own_copy(DOWN, OUT_FAR, c, 1).start()
        own_copy(UP, OUT_NEAR, c, 1).start()
        own_copy(DOWN, OUT_NEAR, c, 0).start()

        def give(i):
            other = c * per_step + i

            @pl.when(other != me)
            def _():
                out_copy(other).start()
        loop(per_step, give)
    loop(CHUNKS, finish)
    new_mom[:, me] = mom_out[:, me]

    def pass_on(c):
        for direction, source, a in ((UP, down, 0), (DOWN, up, 1)):
            own_copy(direction, OUT_FAR, c, a).wait_recv()
            relay_copy(direction, c, source, a).start()
    loop(CHUNKS, pass_on)

    wait_plane(0)
    wait_plane(2)
    wait_plane(3)

    def arrived(c):
        for direction, a in ((UP, 1), (DOWN, 0)):
            own_copy(direction, OUT_NEAR, c, a).wait_recv()

    loop(CHUNKS, arrived)

    def passed_on(c):
        for direction, a in ((UP, 0), (DOWN, 1)):
            relay_copy(direction, c, far, a).wait_recv()
    loop(CHUNKS, passed_on)

    for direction in (UP, DOWN):
        wait_all(new_w.at[:, pl.ds(0, 3 * rows)], z_send.at[direction])


def write_out(new_w, new_mom, out_w, out_mom, sem):
    copies = []
    for a in range(new_w.shape[0]):
        half = new_w.shape[1] // 2
        for part in range(2):
            where = (a, pl.ds(part * half, half))
            copies.append(pltpu.make_async_copy(new_w.at[where], out_w.at[where], sem.at[len(copies)]))
        copies.append(pltpu.make_async_copy(new_mom.at[a], out_mom.at[a], sem.at[len(copies)]))
    for copy in copies:
        copy.start()
    for copy in copies:
        copy.wait()


def body(inner_weights, start_weights, momentum):
    groups, shards, tps = lax.axis_size("grp"), lax.axis_size("shard"), lax.axis_size("tp")
    plane = shards * tps
    mats, row_count, col_count = start_weights.shape
    q_rows = momentum.shape[4]
    quarter = row_count // groups
    any_spec = pl.BlockSpec(memory_space=pl.ANY)
    flat_shape = (mats, plane, q_rows, col_count)
    dma = pltpu.SemaphoreType.DMA
    new_w, new_mom = pl.pallas_call(
        kernel,
        out_shape=(
            pltpu.VMEM(start_weights.shape, jnp.float32),
            pltpu.VMEM(flat_shape, jnp.float32),
        ),
        in_specs=[any_spec] * 3,
        out_specs=(pl.BlockSpec(memory_space=pltpu.VMEM),) * 2,
        scratch_shapes=[
            pltpu.VMEM(start_weights.shape, jnp.float32),
            pltpu.VMEM(start_weights.shape, jnp.float32),
            pltpu.VMEM((2, 3, quarter, col_count), jnp.float32),
            pltpu.VMEM(flat_shape, jnp.float32),
            pltpu.VMEM(flat_shape, jnp.float32),
            dma((4, 2)),
            dma((2,)),
            dma((2, 6, CHUNKS)),
            dma((4,)),
            dma((1,)),
            pltpu.SemaphoreType.REGULAR((2,)),
            pltpu.SemaphoreType.REGULAR((7,)),
        ],
        compiler_params=pltpu.CompilerParams(collective_id=0, has_side_effects=True, vmem_limit_bytes=50000000),
        name="outer_step",
    )(inner_weights[0], start_weights, momentum.reshape(flat_shape))
    vmem_spec = pl.BlockSpec(memory_space=pltpu.VMEM)
    out_w, out_mom = pl.pallas_call(
        write_out,
        out_shape=(
            jax.ShapeDtypeStruct(start_weights.shape, jnp.float32),
            jax.ShapeDtypeStruct(flat_shape, jnp.float32),
        ),
        in_specs=[vmem_spec] * 2,
        out_specs=(any_spec, any_spec),
        scratch_shapes=[dma((6,))],
        compiler_params=pltpu.CompilerParams(vmem_limit_bytes=4000000),
        name="write_out",
    )(new_w, new_mom)
    return out_w, out_mom.reshape(momentum.shape)


def solution(mesh):
    in_specs = (
        P("grp", None, "shard", "tp"),
        P(None, "shard", "tp"),
        P(None, None, None, ("grp", "shard", "tp"), None, None),
    )
    out_specs = (P(None, "shard", "tp"), P(None, None, None, ("grp", "shard", "tp"), None, None))
    return jax.shard_map(body, mesh=mesh, in_specs=in_specs, out_specs=out_specs, check_vma=False)
```

```python
import functools

import jax
import jax.numpy as jnp
from jax import lax
from jax.experimental import pallas as pl
from jax.experimental.pallas import tpu as pltpu
from jax.sharding import PartitionSpec as P

OUTER_RATE = 0.7
MOMENTUM_COEF = 0.5
CHUNKS = 2
UP, DOWN = 0, 1
FAR, NEAR, RELAY, OUT_FAR, OUT_END = 0, 1, 2, 2 + CHUNKS, 2 + 2 * CHUNKS
MESH = pl.DeviceIdType.MESH


def kernel(
    inner, start, mom, new_w, new_mom,
    diff, base, land, mom_in, mom_out,
    load_sem, z_send, z_recv, plane_sem, near_sem, word_sem,
):
    groups, shards, tps = lax.axis_size("grp"), lax.axis_size("shard"), lax.axis_size("tp")
    plane = shards * tps
    g, s, t = lax.axis_index("grp"), lax.axis_index("shard"), lax.axis_index("tp")
    me = s * tps + t
    up, down, far = (g + 1) % groups, (g + groups - 1) % groups, (g + 2) % groups
    rows = start.shape[1] // groups
    step = rows // CHUNKS
    q_rows = mom.shape[2]
    per_step = step // q_rows
    side = ((up, s, t), (down, s, t))

    def at_rows(quarter, c):
        return pl.ds(pl.multiple_of(quarter * rows + c * step, step), step)

    def in_chunk(c):
        return pl.ds(pl.multiple_of(c * step, step), step)

    def whole(quarter):
        return pl.ds(pl.multiple_of(quarter * rows, rows), rows)

    def wait_all(ref, sem):
        pltpu.make_async_copy(ref, ref, sem).wait()

    blocks = ((0, up), (1, down), (0, g), (1, g))

    def subtract(a, quarter):
        def one(c, carry):
            where = at_rows(quarter, c)
            diff[a, where] = base[a, where] - diff[a, where]
            return carry
        lax.fori_loop(0, CHUNKS, one, 0)

    def z_copy(direction, slot, src, dst):
        return pltpu.make_async_remote_copy(
            src_ref=src, dst_ref=dst,
            send_sem=z_send.at[direction], recv_sem=z_recv.at[direction, slot],
            device_id=side[direction], device_id_type=MESH)

    def raw_copy(direction, kind, quarter, a):
        return z_copy(direction, kind, inner.at[a, whole(quarter)], land.at[direction, kind])

    def sum_copy(direction, c, quarter, a):
        slot = land.at[direction, RELAY, in_chunk(c)]
        return z_copy(direction, RELAY + c, diff.at[a, at_rows(quarter, c)], slot)

    def far_copy(direction, c, a):
        where = at_rows(g, c)
        return z_copy(direction, OUT_FAR + c, new_w.at[a, where], new_w.at[a, where])

    def end_copy(direction, quarter, a):
        where = whole(quarter)
        return z_copy(direction, OUT_END, new_w.at[a, where], new_w.at[a, where])

    def partner(k):
        other = (me + k) % plane
        return other, (g, other // tps, other % tps)

    def in_copy(k):
        other, device = partner(k)
        return pltpu.make_async_remote_copy(
            src_ref=mom.at[:, other], dst_ref=mom_in.at[:, me],
            send_sem=plane_sem.at[0], recv_sem=plane_sem.at[1],
            device_id=device, device_id_type=MESH)

    def wait_plane(i):
        wait_all(mom_out.at[:, pl.ds(0, plane - 1)], plane_sem.at[i])

    def out_copy(other):
        return pltpu.make_async_remote_copy(
            src_ref=mom_out.at[:, other], dst_ref=new_mom.at[:, me],
            send_sem=plane_sem.at[2], recv_sem=plane_sem.at[3],
            device_id=(g, other // tps, other % tps), device_id_type=MESH)

    def loop(n, body):
        def one(i, carry):
            body(i)
            return carry
        lax.fori_loop(0, n, one, 0)

    x_size, y_low = shards // 2, tps // 2
    x, y, core = s % x_size, (s // x_size) * y_low + t // 2, t % 2

    def seat(dx, dy, dcore):
        nx, ny = (x + dx + x_size) % x_size, (y + dy + 2 * y_low) % (2 * y_low)
        return (g, (ny // y_low) * x_size + nx, (ny % y_low) * 2 + (core + dcore) % 2)

    along_x, along_y, beside = (seat(1, 0, 0), seat(-1, 0, 0)), (seat(0, 1, 0), seat(0, -1, 0)), (seat(0, 0, 1),)

    def signal(sem, *devices):
        for device in devices:
            pl.semaphore_signal(sem, inc=1, device_id=device, device_id_type=MESH)

    barrier = pltpu.get_barrier_semaphore()

    @pl.when(g == 0)
    def _():
        signal(barrier, *side, *along_x, *along_y, *beside)

    pl.semaphore_wait(barrier, jnp.where(g == 0, 5, jnp.where(g == 2, 2, 1)))


    @pl.when((g == 3) | (g == 2))
    def _():
        signal(near_sem.at[DOWN], side[UP])

    @pl.when((g == 1) | (g == 2))
    def _():
        signal(near_sem.at[UP], side[DOWN])

    @pl.when(g == 3)
    def _():
        signal(barrier, side[DOWN])

    @pl.when(g == 1)
    def _():
        signal(barrier, side[UP])

    def send_raw(direction, a, owner):
        raw_copy(direction, FAR, far, a).start()
        raw_copy(direction, NEAR, owner, 1 - a).start()

    @pl.when(g == 1)
    def _():
        send_raw(DOWN, 1, down)

    @pl.when(g < 2)
    def _():
        pl.semaphore_wait(near_sem.at[UP], 1)
    send_raw(UP, 0, up)

    @pl.when((g == 0) | (g == 3))
    def _():
        pl.semaphore_wait(near_sem.at[DOWN], 1)

    @pl.when(g != 1)
    def _():
        send_raw(DOWN, 1, down)

    @pl.when(g == 1)
    def _():
        signal(word_sem.at[0], side[DOWN])

    rounds = (along_x, along_y, along_x, along_y, beside)

    def hear(i):
        @pl.when(g == 0)
        def _():
            pl.semaphore_wait(word_sem.at[i], 1 if i == 0 else len(rounds[i - 1]))
            if i < len(rounds):
                signal(word_sem.at[i + 1], *rounds[i])
            else:
                signal(word_sem.at[i + 1], (up, s, t), (far, s, t), (down, s, t))

    for a, quarter in blocks:
        for src, dst in ((inner, diff), (start, base)):
            pltpu.make_async_copy(src.at[a, whole(quarter)], dst.at[a, whole(quarter)], load_sem).start()
    pltpu.make_async_copy(mom.at[:, me], mom_in.at[:, me], plane_sem.at[1]).start()

    hear(0)
    wait_all(base, load_sem)
    for i in range(4):
        subtract(*blocks[i])
        hear(i + 1)
    hear(5)

    @pl.when(g != 0)
    def _():
        pl.semaphore_wait(word_sem.at[6], 1)
    loop(plane - 1, lambda k: in_copy(k + 1).start())

    for direction, a in ((UP, 0), (DOWN, 1)):
        raw_copy(direction, FAR, far, a).wait_recv()

    def send_sums(c):
        for direction, a, quarter in ((UP, 0, up), (DOWN, 1, down)):
            where = at_rows(quarter, c)
            diff[a, where] = diff[a, where] + (base[a, where] - land[direction, FAR, in_chunk(c)])
        sum_copy(UP, c, up, 0).start()
        sum_copy(DOWN, c, down, 1).start()
    loop(CHUNKS, send_sums)

    wait_all(mom_in, plane_sem.at[1])
    for direction, a in ((UP, 1), (DOWN, 0)):
        raw_copy(direction, NEAR, far, a).wait_recv()

    def finish(c):
        for direction, a in ((UP, 0), (DOWN, 1)):
            sum_copy(direction, c, up, a).wait_recv()

        def pair(i):
            for a, near, relay in ((0, DOWN, UP), (1, UP, DOWN)):
                local = pl.ds(pl.multiple_of(c * step + i * 2 * q_rows, 2 * q_rows), 2 * q_rows)
                where = pl.ds(pl.multiple_of(g * rows + c * step + i * 2 * q_rows, 2 * q_rows), 2 * q_rows)
                j = c * per_step + 2 * i
                total = diff[a, where] + (base[a, where] - land[near, NEAR, local]) + land[relay, RELAY, local]
                flat = total / groups
                old = jnp.concatenate([mom_in[a, j], mom_in[a, j + 1]], axis=0)
                fresh = MOMENTUM_COEF * old + flat
                mom_out[a, j] = fresh[:q_rows]
                mom_out[a, j + 1] = fresh[q_rows:]
                new_w[a, where] = base[a, where] - OUTER_RATE * (flat + MOMENTUM_COEF * fresh)
        loop(per_step // 2, pair)
        far_copy(UP, c, 0).start()
        far_copy(DOWN, c, 1).start()

        def give(i):
            other = c * per_step + i

            @pl.when(other != me)
            def _():
                out_copy(other).start()
        loop(per_step, give)
    loop(CHUNKS, finish)
    end_copy(UP, g, 1).start()
    end_copy(DOWN, g, 0).start()
    new_mom[:, me] = mom_out[:, me]

    for direction, source, a in ((UP, down, 0), (DOWN, up, 1)):
        loop(CHUNKS, lambda c: far_copy(direction, c, a).wait_recv())
        end_copy(direction, source, a).start()

    wait_plane(0)
    wait_plane(2)
    wait_plane(3)

    for direction in (UP, DOWN):
        wait_all(new_w.at[:, whole(0)], z_recv.at[direction, OUT_END])
    for direction in (UP, DOWN):
        wait_all(new_w.at[:, pl.ds(0, 3 * rows)], z_send.at[direction])


def write_out(new_w, new_mom, out_w, out_mom, sem):
    copies = []
    for a in range(new_w.shape[0]):
        half = new_w.shape[1] // 2
        for part in range(2):
            where = (a, pl.ds(part * half, half))
            copies.append(pltpu.make_async_copy(new_w.at[where], out_w.at[where], sem.at[len(copies)]))
        copies.append(pltpu.make_async_copy(new_mom.at[a], out_mom.at[a], sem.at[len(copies)]))
    for copy in copies:
        copy.start()
    for copy in copies:
        copy.wait()


def body(inner_weights, start_weights, momentum):
    groups, shards, tps = lax.axis_size("grp"), lax.axis_size("shard"), lax.axis_size("tp")
    plane = shards * tps
    mats, row_count, col_count = start_weights.shape
    q_rows = momentum.shape[4]
    quarter = row_count // groups
    any_spec = pl.BlockSpec(memory_space=pl.ANY)
    flat_shape = (mats, plane, q_rows, col_count)
    dma = pltpu.SemaphoreType.DMA
    new_w, new_mom = pl.pallas_call(
        kernel,
        out_shape=(
            pltpu.VMEM(start_weights.shape, jnp.float32),
            pltpu.VMEM(flat_shape, jnp.float32),
        ),
        in_specs=[any_spec] * 3,
        out_specs=(pl.BlockSpec(memory_space=pltpu.VMEM),) * 2,
        scratch_shapes=[
            pltpu.VMEM(start_weights.shape, jnp.float32),
            pltpu.VMEM(start_weights.shape, jnp.float32),
            pltpu.VMEM((2, 3, quarter, col_count), jnp.float32),
            pltpu.VMEM(flat_shape, jnp.float32),
            pltpu.VMEM(flat_shape, jnp.float32),
            dma,
            dma((2,)),
            dma((2, 3 + 2 * CHUNKS)),
            dma((4,)),
            pltpu.SemaphoreType.REGULAR((2,)),
            pltpu.SemaphoreType.REGULAR((7,)),
        ],
        compiler_params=pltpu.CompilerParams(collective_id=0, has_side_effects=True, vmem_limit_bytes=50000000),
        name="outer_step",
    )(inner_weights[0], start_weights, momentum.reshape(flat_shape))
    vmem_spec = pl.BlockSpec(memory_space=pltpu.VMEM)
    out_w, out_mom = pl.pallas_call(
        write_out,
        out_shape=(
            jax.ShapeDtypeStruct(start_weights.shape, jnp.float32),
            jax.ShapeDtypeStruct(flat_shape, jnp.float32),
        ),
        in_specs=[vmem_spec] * 2,
        out_specs=(any_spec, any_spec),
        scratch_shapes=[dma((6,))],
        compiler_params=pltpu.CompilerParams(vmem_limit_bytes=4000000),
        name="write_out",
    )(new_w, new_mom)
    return out_w, out_mom.reshape(momentum.shape)


def solution(mesh):
    in_specs = (
        P("grp", None, "shard", "tp"),
        P(None, "shard", "tp"),
        P(None, None, None, ("grp", "shard", "tp"), None, None),
    )
    out_specs = (P(None, "shard", "tp"), P(None, None, None, ("grp", "shard", "tp"), None, None))
    return jax.shard_map(body, mesh=mesh, in_specs=in_specs, out_specs=out_specs, check_vma=False)
```

```python
import functools

import jax
import jax.numpy as jnp
from jax import lax
from jax.experimental import pallas as pl
from jax.experimental.pallas import tpu as pltpu
from jax.sharding import PartitionSpec as P

OUTER_RATE = 0.7
MOMENTUM_COEF = 0.5
CHUNKS = 4
UP, DOWN = 0, 1
FAR, NEAR, RELAY, OUT_FAR, OUT_END = 0, 1, 2, 2 + CHUNKS, 2 + 2 * CHUNKS
MESH = pl.DeviceIdType.MESH


def kernel(
    inner, start, mom, new_w, new_mom,
    diff, base, land, mom_in, mom_out,
    load_sem, z_send, z_recv, plane_sem, near_sem, word_sem,
):
    groups, shards, tps = lax.axis_size("grp"), lax.axis_size("shard"), lax.axis_size("tp")
    plane = shards * tps
    g, s, t = lax.axis_index("grp"), lax.axis_index("shard"), lax.axis_index("tp")
    me = s * tps + t
    up, down, far = (g + 1) % groups, (g + groups - 1) % groups, (g + 2) % groups
    rows = start.shape[1] // groups
    step = rows // CHUNKS
    q_rows = mom.shape[2]
    per_step = step // q_rows
    side = ((up, s, t), (down, s, t))

    def at_rows(quarter, c):
        return pl.ds(pl.multiple_of(quarter * rows + c * step, step), step)

    def in_chunk(c):
        return pl.ds(pl.multiple_of(c * step, step), step)

    def whole(quarter):
        return pl.ds(pl.multiple_of(quarter * rows, rows), rows)

    def wait_all(ref, sem):
        pltpu.make_async_copy(ref, ref, sem).wait()

    blocks = ((0, up), (1, down), (0, g), (1, g))

    def subtract(a, quarter):
        def one(c, carry):
            where = at_rows(quarter, c)
            diff[a, where] = base[a, where] - diff[a, where]
            return carry
        lax.fori_loop(0, CHUNKS, one, 0)

    def z_copy(direction, slot, src, dst):
        return pltpu.make_async_remote_copy(
            src_ref=src, dst_ref=dst,
            send_sem=z_send.at[direction], recv_sem=z_recv.at[direction, slot],
            device_id=side[direction], device_id_type=MESH)

    def raw_copy(direction, kind, quarter, a):
        return z_copy(direction, kind, inner.at[a, whole(quarter)], land.at[direction, kind])

    def sum_copy(direction, c, quarter, a):
        slot = land.at[direction, RELAY, in_chunk(c)]
        return z_copy(direction, RELAY + c, diff.at[a, at_rows(quarter, c)], slot)

    def far_copy(direction, c, a):
        where = at_rows(g, c)
        return z_copy(direction, OUT_FAR + c, new_w.at[a, where], new_w.at[a, where])

    def end_copy(direction, quarter, a):
        where = whole(quarter)
        return z_copy(direction, OUT_END, new_w.at[a, where], new_w.at[a, where])

    def partner(k):
        other = (me + k) % plane
        return other, (g, other // tps, other % tps)

    def in_copy(k):
        other, device = partner(k)
        return pltpu.make_async_remote_copy(
            src_ref=mom.at[:, other], dst_ref=mom_in.at[:, me],
            send_sem=plane_sem.at[0], recv_sem=plane_sem.at[1],
            device_id=device, device_id_type=MESH)

    def wait_plane(i):
        wait_all(mom_out.at[:, pl.ds(0, plane - 1)], plane_sem.at[i])

    def out_copy(other):
        return pltpu.make_async_remote_copy(
            src_ref=mom_out.at[:, other], dst_ref=new_mom.at[:, me],
            send_sem=plane_sem.at[2], recv_sem=plane_sem.at[3],
            device_id=(g, other // tps, other % tps), device_id_type=MESH)

    def loop(n, body):
        def one(i, carry):
            body(i)
            return carry
        lax.fori_loop(0, n, one, 0)

    x_size, y_low = shards // 2, tps // 2
    x, y, core = s % x_size, (s // x_size) * y_low + t // 2, t % 2

    def seat(dx, dy, dcore):
        nx, ny = (x + dx + x_size) % x_size, (y + dy + 2 * y_low) % (2 * y_low)
        return (g, (ny // y_low) * x_size + nx, (ny % y_low) * 2 + (core + dcore) % 2)

    along_x, along_y, beside = (seat(1, 0, 0), seat(-1, 0, 0)), (seat(0, 1, 0), seat(0, -1, 0)), (seat(0, 0, 1),)

    def signal(sem, *devices):
        for device in devices:
            pl.semaphore_signal(sem, inc=1, device_id=device, device_id_type=MESH)

    barrier = pltpu.get_barrier_semaphore()

    @pl.when(g == 0)
    def _():
        signal(barrier, *side, *along_x, *along_y, *beside)

    pl.semaphore_wait(barrier, jnp.where(g == 0, 5, jnp.where(g == 2, 2, 1)))


    @pl.when((g == 3) | (g == 2))
    def _():
        signal(near_sem.at[DOWN], side[UP])

    @pl.when((g == 1) | (g == 2))
    def _():
        signal(near_sem.at[UP], side[DOWN])

    @pl.when(g == 3)
    def _():
        signal(barrier, side[DOWN])

    @pl.when(g == 1)
    def _():
        signal(barrier, side[UP])

    def send_raw(direction, a, owner):
        raw_copy(direction, FAR, far, a).start()
        raw_copy(direction, NEAR, owner, 1 - a).start()

    @pl.when(g == 1)
    def _():
        send_raw(DOWN, 1, down)

    @pl.when(g < 2)
    def _():
        pl.semaphore_wait(near_sem.at[UP], 1)
    send_raw(UP, 0, up)

    @pl.when((g == 0) | (g == 3))
    def _():
        pl.semaphore_wait(near_sem.at[DOWN], 1)

    @pl.when(g != 1)
    def _():
        send_raw(DOWN, 1, down)

    @pl.when(g == 1)
    def _():
        signal(word_sem.at[0], side[DOWN])

    rounds = (along_x, along_y, along_x, along_y, beside)

    def hear(i):
        @pl.when(g == 0)
        def _():
            pl.semaphore_wait(word_sem.at[i], 1 if i == 0 else len(rounds[i - 1]))
            if i < len(rounds):
                signal(word_sem.at[i + 1], *rounds[i])
            else:
                signal(word_sem.at[i + 1], (up, s, t), (far, s, t), (down, s, t))

    for a, quarter in blocks:
        for src, dst in ((inner, diff), (start, base)):
            pltpu.make_async_copy(src.at[a, whole(quarter)], dst.at[a, whole(quarter)], load_sem).start()
    pltpu.make_async_copy(mom.at[:, me], mom_in.at[:, me], plane_sem.at[1]).start()

    hear(0)
    wait_all(base, load_sem)
    for i in range(4):
        subtract(*blocks[i])
        hear(i + 1)
    hear(5)

    @pl.when(g != 0)
    def _():
        pl.semaphore_wait(word_sem.at[6], 1)
    loop(plane - 1, lambda k: in_copy(k + 1).start())

    for direction, a in ((UP, 0), (DOWN, 1)):
        raw_copy(direction, FAR, far, a).wait_recv()

    def send_sums(c):
        for direction, a, quarter in ((UP, 0, up), (DOWN, 1, down)):
            where = at_rows(quarter, c)
            diff[a, where] = diff[a, where] + (base[a, where] - land[direction, FAR, in_chunk(c)])
        sum_copy(UP, c, up, 0).start()
        sum_copy(DOWN, c, down, 1).start()
    loop(CHUNKS, send_sums)

    wait_all(mom_in, plane_sem.at[1])
    for direction, a in ((UP, 1), (DOWN, 0)):
        raw_copy(direction, NEAR, far, a).wait_recv()

    def finish(c):
        for direction, a in ((UP, 0), (DOWN, 1)):
            sum_copy(direction, c, up, a).wait_recv()

        def pair(i):
            for a, near, relay in ((0, DOWN, UP), (1, UP, DOWN)):
                local = pl.ds(pl.multiple_of(c * step + i * 2 * q_rows, 2 * q_rows), 2 * q_rows)
                where = pl.ds(pl.multiple_of(g * rows + c * step + i * 2 * q_rows, 2 * q_rows), 2 * q_rows)
                j = c * per_step + 2 * i
                total = diff[a, where] + (base[a, where] - land[near, NEAR, local]) + land[relay, RELAY, local]
                flat = total / groups
                old = jnp.concatenate([mom_in[a, j], mom_in[a, j + 1]], axis=0)
                fresh = MOMENTUM_COEF * old + flat
                mom_out[a, j] = fresh[:q_rows]
                mom_out[a, j + 1] = fresh[q_rows:]
                new_w[a, where] = base[a, where] - OUTER_RATE * (flat + MOMENTUM_COEF * fresh)
        loop(per_step // 2, pair)
        far_copy(UP, c, 0).start()
        far_copy(DOWN, c, 1).start()

        def give(i):
            other = c * per_step + i

            @pl.when(other != me)
            def _():
                out_copy(other).start()
        loop(per_step, give)
    loop(CHUNKS, finish)
    end_copy(UP, g, 1).start()
    end_copy(DOWN, g, 0).start()
    new_mom[:, me] = mom_out[:, me]

    for direction, source, a in ((UP, down, 0), (DOWN, up, 1)):
        loop(CHUNKS, lambda c: far_copy(direction, c, a).wait_recv())
        end_copy(direction, source, a).start()

    wait_plane(0)
    wait_plane(2)
    wait_plane(3)

    for direction in (UP, DOWN):
        wait_all(new_w.at[:, whole(0)], z_recv.at[direction, OUT_END])
    for direction in (UP, DOWN):
        wait_all(new_w.at[:, pl.ds(0, 3 * rows)], z_send.at[direction])


def write_out(new_w, new_mom, out_w, out_mom, sem):
    copies = []
    for a in range(new_w.shape[0]):
        half = new_w.shape[1] // 2
        for part in range(2):
            where = (a, pl.ds(part * half, half))
            copies.append(pltpu.make_async_copy(new_w.at[where], out_w.at[where], sem.at[len(copies)]))
        copies.append(pltpu.make_async_copy(new_mom.at[a], out_mom.at[a], sem.at[len(copies)]))
    for copy in copies:
        copy.start()
    for copy in copies:
        copy.wait()


def body(inner_weights, start_weights, momentum):
    groups, shards, tps = lax.axis_size("grp"), lax.axis_size("shard"), lax.axis_size("tp")
    plane = shards * tps
    mats, row_count, col_count = start_weights.shape
    q_rows = momentum.shape[4]
    quarter = row_count // groups
    any_spec = pl.BlockSpec(memory_space=pl.ANY)
    flat_shape = (mats, plane, q_rows, col_count)
    dma = pltpu.SemaphoreType.DMA
    new_w, new_mom = pl.pallas_call(
        kernel,
        out_shape=(
            pltpu.VMEM(start_weights.shape, jnp.float32),
            pltpu.VMEM(flat_shape, jnp.float32),
        ),
        in_specs=[any_spec] * 3,
        out_specs=(pl.BlockSpec(memory_space=pltpu.VMEM),) * 2,
        scratch_shapes=[
            pltpu.VMEM(start_weights.shape, jnp.float32),
            pltpu.VMEM(start_weights.shape, jnp.float32),
            pltpu.VMEM((2, 3, quarter, col_count), jnp.float32),
            pltpu.VMEM(flat_shape, jnp.float32),
            pltpu.VMEM(flat_shape, jnp.float32),
            dma,
            dma((2,)),
            dma((2, 3 + 2 * CHUNKS)),
            dma((4,)),
            pltpu.SemaphoreType.REGULAR((2,)),
            pltpu.SemaphoreType.REGULAR((7,)),
        ],
        compiler_params=pltpu.CompilerParams(collective_id=0, has_side_effects=True, vmem_limit_bytes=50000000),
        name="outer_step",
    )(inner_weights[0], start_weights, momentum.reshape(flat_shape))
    vmem_spec = pl.BlockSpec(memory_space=pltpu.VMEM)
    out_w, out_mom = pl.pallas_call(
        write_out,
        out_shape=(
            jax.ShapeDtypeStruct(start_weights.shape, jnp.float32),
            jax.ShapeDtypeStruct(flat_shape, jnp.float32),
        ),
        in_specs=[vmem_spec] * 2,
        out_specs=(any_spec, any_spec),
        scratch_shapes=[dma((6,))],
        compiler_params=pltpu.CompilerParams(vmem_limit_bytes=4000000),
        name="write_out",
    )(new_w, new_mom)
    return out_w, out_mom.reshape(momentum.shape)


def solution(mesh):
    in_specs = (
        P("grp", None, "shard", "tp"),
        P(None, "shard", "tp"),
        P(None, None, None, ("grp", "shard", "tp"), None, None),
    )
    out_specs = (P(None, "shard", "tp"), P(None, None, None, ("grp", "shard", "tp"), None, None))
    return jax.shard_map(body, mesh=mesh, in_specs=in_specs, out_specs=out_specs, check_vma=False)
```
